32 devices in a mesh: rep: 2 (over y), shard: 16 (over z, x, core).
Axes of the slice: x: 2, y: 2, z: 4, core: 2. Of those that a mesh axis runs over, the one named last changes fastest.
Arguments:
- images: bfloat16 [32, 14, 14, 512], P(('rep', 'shard')), may hold values from -6 to 6
- cotangent: bfloat16 [32, 14, 14, 512], P(('rep', 'shard')), may hold values from -6 to 6
- regions: int32 [32, 14, 14], P(('rep', 'shard')), may hold values from 0 to 8, as said below
- w_qkv: bfloat16 [2, 512, 1536], P(None, 'shard'), may hold values from -0.25 to 0.25
- w_proj: bfloat16 [2, 512, 512], P(None, 'shard'), may hold values from -0.75 to 0.75
- w_fc1: bfloat16 [2, 512, 2048], P(None, 'shard'), may hold values from -0.25 to 0.25
- w_fc2: bfloat16 [2, 2048, 512], P(None, 'shard'), may hold values from -0.125 to 0.125
- norm_gains: bfloat16 [2, 2, 512], P(None, None, 'shard'), may hold values from 0.5 to 1.5
- norm_shifts: bfloat16 [2, 2, 512], P(None, None, 'shard'), may hold values from -1.1953125 to 1.1953125
- branch_biases: bfloat16 [2, 4, 512], P(None, None, 'shard'), may hold values from -1.1953125 to 1.1953125
- fc1_bias: bfloat16 [2, 2048], P(None, 'shard'), may hold values from -1.1953125 to 1.1953125
- rel_table: bfloat16 [2, 169, 16], replicated, may hold values from -6 to 6
Outputs:
- images_out: bfloat16 [32, 14, 14, 512], P(('rep', 'shard'))
- images_grad: float32 [32, 14, 14, 512], P(('rep', 'shard'))
- grad_w_qkv: float32 [2, 512, 1536], P(None, 'shard')
- grad_w_proj: float32 [2, 512, 512], P(None, 'shard')
- grad_w_fc1: float32 [2, 512, 2048], P(None, 'shard')
- grad_w_fc2: float32 [2, 2048, 512], P(None, 'shard')
- grad_norm_gains: float32 [2, 2, 512], P(None, None, 'shard')
- grad_norm_shifts: float32 [2, 2, 512], P(None, None, 'shard')
- grad_branch_biases: float32 [2, 4, 512], P(None, None, 'shard')
- grad_fc1_bias: float32 [2, 2048], P(None, 'shard')
- grad_rel_table: float32 [2, 169, 16], replicated
The draws below stay inside these ranges and needn't reach their ends.
Inputs may be any that keep to these rules, and one draw needn't show every extreme that they name: `regions`: in each image the ids are 3 * (row band) + (column band), the rows and the columns each cut into three bands of consecutive positions.
All inputs are finite; a program needn't handle non-finite values.
Results may differ from the reference program's by a relative error of at most 0.023.
Values may be sent and summed in bfloat16 or wider, within the bound.
A program may use at most 128 MiB of HBM per device.

```python
import jax
import jax.numpy as jnp
from jax import lax

D = 512
HEADS = 16
FF = 2048
SIDE = 14
WIN = 7
SHIFT = 3
LAYERS = 2
TABLE = 169
IMAGES = 32


def draw_regions(key, part):
    keys = jax.random.split(key, 4)
    row_first = jax.random.randint(keys[0], (IMAGES, 1, 1), 5, 9)
    row_second = jax.random.randint(keys[1], (IMAGES, 1, 1), 9, 14)
    col_first = jax.random.randint(keys[2], (IMAGES, 1, 1), 5, 9)
    col_second = jax.random.randint(keys[3], (IMAGES, 1, 1), 9, 14)
    row_ids = jnp.arange(SIDE, dtype=jnp.int32)[None, :, None]
    col_ids = jnp.arange(SIDE, dtype=jnp.int32)[None, None, :]
    row_band = (row_ids >= row_first).astype(jnp.int32) + (row_ids >= row_second).astype(jnp.int32)
    col_band = (col_ids >= col_first).astype(jnp.int32) + (col_ids >= col_second).astype(jnp.int32)
    return (3 * row_band + col_band).astype(jnp.int32)


def levels(own_key, dims, cuts, low, high):
    factor_of, own = 1.0, jax.random.fold_in(own_key, 6)
    for dim, shards_of in cuts:
        heights = jnp.exp(jax.random.uniform(jax.random.fold_in(own, dim), (shards_of,), jnp.float32, low / len(cuts), high / len(cuts)))
        factor_of = factor_of * jnp.repeat(heights, dims[dim] // shards_of).reshape([-1 if axis == dim else 1 for axis in range(len(dims))])
    return factor_of


def bell_draw(own_key, dims, width, bound, cuts=(), held_as=jnp.bfloat16):
    loudness = levels(own_key, dims, cuts, -0.22, 0.18) if cuts else 1.0
    drawn = jax.random.normal(own_key, dims, jnp.float32) * width * loudness
    return jnp.minimum(jnp.maximum(drawn, -bound), bound).astype(held_as)


def setup_inputs(seed: int = 0) -> dict:
    key_of = jax.random.split(jax.random.key(seed), 13)
    return {
        "images": bell_draw(key_of[0], (IMAGES, SIDE, SIDE, D), 1.0, 6.0, ((0, 32),)),
        "cotangent": bell_draw(key_of[1], (IMAGES, SIDE, SIDE, D), 1.0, 6.0, ((0, 32),)),
        "regions": draw_regions(jax.random.fold_in(key_of[12], 71), 0),
        "w_qkv": bell_draw(key_of[3], (LAYERS, D, 3 * D), D ** -0.5, 0.25, ((1, 16),)),
        "w_proj": bell_draw(key_of[4], (LAYERS, D, D), (D // 7) ** -0.5, 0.75, ((1, 16),)),
        "w_fc1": bell_draw(key_of[5], (LAYERS, D, FF), D ** -0.5, 0.25, ((1, 16),)),
        "w_fc2": bell_draw(key_of[6], (LAYERS, FF, D), FF ** -0.5, 0.125, ((1, 16),)),
        "norm_gains": jnp.clip(1.0 + 0.1 * jax.random.normal(key_of[7], (LAYERS, 2, D), jnp.float32), 0.5, 1.5).astype(jnp.bfloat16),
        "norm_shifts": bell_draw(key_of[8], (LAYERS, 2, D), 0.2, 1.1953125, ((2, 16),)),
        "branch_biases": bell_draw(key_of[9], (LAYERS, 4, D), 0.2, 1.1953125, ((2, 16),)),
        "fc1_bias": bell_draw(key_of[10], (LAYERS, FF), 0.2, 1.1953125, ((1, 16),)),
        "rel_table": bell_draw(key_of[11], (LAYERS, TABLE, HEADS), 1.0, 6.0),
    }


@jax.custom_vjp
def low(v):
    return lax.optimization_barrier(v.astype(jnp.bfloat16)).astype(jnp.float32)

@jax.custom_vjp
def low_back(v):
    return v

def low_keep(v):
    return (low(v), None)

def low_pass(kept, grad):
    return (grad,)

def back_keep(v):
    return (v, None)

def back_low(kept, grad):
    return (low(grad),)
low.defvjp(low_keep, low_pass)
low_back.defvjp(back_keep, back_low)
eps = 1e-05
highest = lax.Precision.HIGHEST

def layer_norm(values, norm_gain, norm_shift):
    row_mean = lax.optimization_barrier(jnp.mean(values, axis=-1, keepdims=True))
    centred = values - row_mean
    row_var = lax.optimization_barrier(jnp.mean(centred * centred, axis=-1, keepdims=True))
    return centred * lax.rsqrt(row_var + eps) * norm_gain + norm_shift

def to_windows(grid_data):
    image_count = grid_data.shape[0]
    per_side = SIDE // WIN
    trailing = grid_data.shape[3:]
    blocks = grid_data.reshape((image_count, per_side, WIN, per_side, WIN) + trailing)
    blocks = jnp.swapaxes(blocks, 2, 3)
    return blocks.reshape((image_count * per_side * per_side, WIN * WIN) + trailing)

def from_windows(blocks, image_count):
    per_side = SIDE // WIN
    trailing = blocks.shape[2:]
    grid_data = blocks.reshape((image_count, per_side, per_side, WIN, WIN) + trailing)
    grid_data = jnp.swapaxes(grid_data, 2, 3)
    return grid_data.reshape((image_count, SIDE, SIDE) + trailing)

def relative_index():
    cell_ids = jnp.arange(WIN * WIN)
    cell_row = cell_ids // WIN
    cell_col = cell_ids % WIN
    table_side = 2 * WIN - 1
    rel_index = (cell_row[:, None] - cell_row[None, :] + WIN - 1) * table_side + (cell_col[:, None] - cell_col[None, :] + WIN - 1)
    return rel_index.reshape(-1)

def forward(residual, params, regions):
    w_qkv, w_proj, w_fc1, w_fc2, gains, shifts, biases, fc1_bias, table = params
    image_count = residual.shape[0]
    model_width = w_proj.shape[2]
    head_count = table.shape[2]
    head_dim = model_width // head_count
    rel_index = relative_index()
    region_win = to_windows(regions)
    same_region = region_win[:, :, None] == region_win[:, None, :]
    region_mask = jnp.where(same_region, 0.0, -100.0).astype(jnp.float32)
    for layer_num in range(w_qkv.shape[0]):
        shifted = layer_num % 2 == 1
        normed = low(layer_norm(residual, gains[layer_num, 0], shifts[layer_num, 0]))
        if shifted:
            normed = jnp.roll(normed, (-SHIFT, -SHIFT), axis=(1, 2))
        window_rows = to_windows(normed)
        window_count = window_rows.shape[0]
        projected = jnp.einsum('nti,ij->ntj', window_rows, w_qkv[layer_num], precision=highest)
        queries = low(low_back((projected[..., :model_width] + biases[layer_num, 0]) * head_dim ** (-0.5)))
        key_rows = low(low_back(projected[..., model_width:2 * model_width]))
        values = low(low_back(projected[..., 2 * model_width:] + biases[layer_num, 1]))
        queries = queries.reshape(window_count, WIN * WIN, head_count, head_dim)
        key_rows = key_rows.reshape(window_count, WIN * WIN, head_count, head_dim)
        values = values.reshape(window_count, WIN * WIN, head_count, head_dim)
        score_bias = table[layer_num][rel_index].T.reshape(head_count, WIN * WIN, WIN * WIN)
        scores = jnp.einsum('nqhd,nkhd->nhqk', queries, key_rows, precision=highest) + score_bias[None]
        if shifted:
            scores = scores + region_mask[:, None]
        scores = low_back(scores)
        attn_probs = low(jax.nn.softmax(scores, axis=-1))
        mixed_rows = jnp.einsum('nhqk,nkhd->nqhd', attn_probs, values, precision=highest)
        mixed_rows = low(low_back(mixed_rows.reshape(window_count, WIN * WIN, model_width)))
        branch = jnp.einsum('nti,ij->ntj', mixed_rows, w_proj[layer_num], precision=highest) + biases[layer_num, 2]
        branch = from_windows(low_back(branch), image_count)
        if shifted:
            branch = jnp.roll(branch, (SHIFT, SHIFT), axis=(1, 2))
        residual = residual + branch
        normed = low(layer_norm(residual, gains[layer_num, 1], shifts[layer_num, 1]))
        pre_act = low_back(jnp.einsum('...i,ij->...j', normed, w_fc1[layer_num], precision=highest) + fc1_bias[layer_num])
        activated = low(jax.nn.gelu(pre_act, approximate=False))
        mlp_out = low_back(jnp.einsum('...i,ij->...j', activated, w_fc2[layer_num], precision=highest) + biases[layer_num, 3])
        residual = residual + mlp_out
    return residual

def reference(images, cotangent, regions, w_qkv, w_proj, w_fc1, w_fc2, norm_gains, norm_shifts, branch_biases, fc1_bias, rel_table):
    params = tuple((p.astype(jnp.float32) for p in (w_qkv, w_proj, w_fc1, w_fc2, norm_gains, norm_shifts, branch_biases, fc1_bias, rel_table)))
    group_size = 16
    group_count = images.shape[0] // group_size

    def regroup(array):
        return array.reshape((group_count, group_size) + array.shape[1:])

    def group_step(grad_total, group_data):
        inputs, cot_rows, region_rows = group_data

        def run(values, weights):
            return forward(values, weights, region_rows)
        result, pullback = jax.vjp(run, inputs.astype(jnp.float32), params)
        grad_input, grad_params = pullback(cot_rows.astype(jnp.float32))
        grad_total = jax.tree.map(lambda a, b: a + b, grad_total, grad_params)
        return (grad_total, (result.astype(jnp.bfloat16), grad_input))
    zero_grads = tuple((jnp.zeros_like(p) for p in params))
    grad_total, (results, grad_inputs) = lax.scan(group_step, zero_grads, (regroup(images), regroup(cotangent), regroup(regions)))
    return (results.reshape(images.shape), grad_inputs.reshape(images.shape), grad_total[0], grad_total[1], grad_total[2], grad_total[3], grad_total[4], grad_total[5], grad_total[6], grad_total[7], grad_total[8])
```

```python
import functools

import jax
import jax.numpy as jnp
from jax import lax
from jax.sharding import PartitionSpec as P

SIDE = 14
WIN = 7
SHIFT = 3
PAD_ROWS = 16


eps = 1e-05
highest = lax.Precision.HIGHEST
inv_root_two = 0.7071067811865476
inv_root_two_pi = 0.3989422804014327


def layer_norm(values, norm_gain, norm_shift):
    row_mean = jnp.mean(values, axis=-1, keepdims=True)
    centred = values - row_mean
    row_var = jnp.mean(centred * centred, axis=-1, keepdims=True)
    return centred * lax.rsqrt(row_var + eps) * norm_gain + norm_shift


def times_transposed(left, right):
    return lax.dot_general(
        left, right, (((1,), (1,)), ((), ())), preferred_element_type=jnp.float32
    )


def transposed_times(left, right):
    return lax.dot_general(
        left, right, (((0,), (0,)), ((), ())), preferred_element_type=jnp.float32
    )


def gelu_slope(pre_act):
    return 0.5 * (1.0 + lax.erf(pre_act * inv_root_two)) + pre_act * inv_root_two_pi * jnp.exp(
        -0.5 * pre_act * pre_act
    )


def to_windows(grid_data):
    image_count = grid_data.shape[0]
    per_side = SIDE // WIN
    trailing = grid_data.shape[3:]
    blocks = grid_data.reshape((image_count, per_side, WIN, per_side, WIN) + trailing)
    blocks = jnp.swapaxes(blocks, 2, 3)
    return blocks.reshape((image_count * per_side * per_side, WIN * WIN) + trailing)


def from_windows(blocks, image_count):
    per_side = SIDE // WIN
    trailing = blocks.shape[2:]
    grid_data = blocks.reshape((image_count, per_side, per_side, WIN, WIN) + trailing)
    grid_data = jnp.swapaxes(grid_data, 2, 3)
    return grid_data.reshape((image_count, SIDE, SIDE) + trailing)


def onehot_table():
    cell_ids = jnp.arange(WIN * WIN)
    cell_row = cell_ids // WIN
    cell_col = cell_ids % WIN
    table_side = 2 * WIN - 1
    rel_index = (cell_row[:, None] - cell_row[None, :] + WIN - 1) * table_side + (
        cell_col[:, None] - cell_col[None, :] + WIN - 1
    )
    rel_index = rel_index.reshape(-1)
    return (rel_index[:, None] == jnp.arange(table_side * table_side)[None, :]).astype(jnp.float32)


def pack_local(w_qkv, w_proj, w_fc1, w_fc2, gains, shifts, biases, fc1_bias):
    width = w_proj.shape[1]
    blocks = [w_qkv[:, n * width : (n + 1) * width] for n in range(w_qkv.shape[1] // width)]
    blocks.append(w_proj)
    blocks += [w_fc1[:, n * width : (n + 1) * width] for n in range(w_fc1.shape[1] // width)]
    blocks.append(w_fc2)
    small = jnp.concatenate(
        [gains.reshape(-1), shifts.reshape(-1), biases.reshape(-1), fc1_bias.reshape(-1)]
    )
    small = jnp.pad(small, (0, width - small.shape[0])).reshape(1, width)
    blocks.append(jnp.pad(small, ((0, PAD_ROWS - 1), (0, 0))))
    return jnp.concatenate(blocks, axis=0)


def unpack_gathered(packed, w_qkv, w_fc1, w_fc2):
    shard_count, _, width = packed.shape
    rows = w_qkv.shape[0]
    full = rows * shard_count

    def piece(n):
        return packed[:, n * rows : (n + 1) * rows].reshape(full, width)

    qkv_parts = w_qkv.shape[1] // width
    fc1_parts = w_fc1.shape[1] // width
    wqkv = jnp.concatenate([piece(n) for n in range(qkv_parts)], axis=1)
    wproj = piece(qkv_parts)
    wfirst = jnp.concatenate([piece(qkv_parts + 1 + n) for n in range(fc1_parts)], axis=1)
    start = (qkv_parts + 1 + fc1_parts) * rows
    wsecond = packed[:, start : start + w_fc2.shape[0]].reshape(-1, width)
    small = packed[:, start + w_fc2.shape[0]]

    def vectors(first, count):
        part = small[:, first : first + count * rows].reshape(shard_count, count, rows)
        return jnp.swapaxes(part, 0, 1).reshape(count, full)

    gains, shifts, biases = vectors(0, 2), vectors(2 * rows, 2), vectors(4 * rows, 4)
    bias_first = small[:, 8 * rows : 8 * rows + w_fc2.shape[0]].reshape(-1)
    return (wqkv, wproj, gains, shifts, biases), (wfirst, wsecond, bias_first)


def pack_grads(qkv, proj, first, second, gains, shifts, biases, bias_first, shard_count):
    width = proj.shape[1]

    def rows_of(block):
        return block.astype(jnp.bfloat16).reshape(shard_count, -1, block.shape[-1])

    def vectors(block):
        split = block.reshape(block.shape[0], shard_count, -1)
        return jnp.swapaxes(split, 0, 1).reshape(shard_count, -1)

    blocks = [rows_of(qkv[:, n * width : (n + 1) * width]) for n in range(qkv.shape[1] // width)]
    blocks.append(rows_of(proj))
    blocks += [rows_of(first[:, n * width : (n + 1) * width]) for n in range(first.shape[1] // width)]
    blocks.append(rows_of(second))
    small = jnp.concatenate(
        [vectors(gains), vectors(shifts), vectors(biases), bias_first.reshape(shard_count, -1)],
        axis=1,
    ).astype(jnp.bfloat16)
    small = jnp.pad(small, ((0, 0), (0, width - small.shape[1])))[:, None]
    blocks.append(jnp.pad(small, ((0, 0), (0, PAD_ROWS - 1), (0, 0))))
    return jnp.concatenate(blocks, axis=1)


def rep_sum(share, rep_count):
    total = share
    step = 1
    while step < rep_count:
        pairs = [(n, n ^ step) for n in range(rep_count)]
        total = total + lax.ppermute(total, "rep", pairs)
        step *= 2
    return total


def unpack_shares(shares, w_qkv, w_fc2, fc1_bias):
    shares = shares.astype(jnp.float32)
    layer_count, _, width = shares.shape
    rows = w_qkv.shape[1]
    hidden = fc1_bias.shape[1]
    qkv_parts = w_qkv.shape[2] // width
    fc1_parts = (shares.shape[1] - PAD_ROWS - w_fc2.shape[1]) // rows - qkv_parts - 1

    def piece(n):
        return shares[:, n * rows : (n + 1) * rows]

    start = (qkv_parts + 1 + fc1_parts) * rows
    small = shares[:, start + w_fc2.shape[1]]
    return (
        jnp.concatenate([piece(n) for n in range(qkv_parts)], axis=2),
        piece(qkv_parts),
        jnp.concatenate([piece(qkv_parts + 1 + n) for n in range(fc1_parts)], axis=2),
        shares[:, start : start + w_fc2.shape[1]],
        small[:, : 2 * rows].reshape(layer_count, 2, rows),
        small[:, 2 * rows : 4 * rows].reshape(layer_count, 2, rows),
        small[:, 4 * rows : 8 * rows].reshape(layer_count, 4, rows),
        small[:, 8 * rows : 8 * rows + hidden],
    )


def body(
    images,
    cotangent,
    regions,
    w_qkv,
    w_proj,
    w_fc1,
    w_fc2,
    norm_gains,
    norm_shifts,
    branch_biases,
    fc1_bias,
    rel_table,
    rep_count,
    shard_count,
):
    layer_count = w_qkv.shape[0]
    image_count = images.shape[0]
    model_width = w_proj.shape[2]
    head_count = rel_table.shape[2]
    head_dim = model_width // head_count
    query_scale = head_dim ** (-0.5)
    column_scale = jnp.concatenate(
        [
            jnp.full((model_width,), query_scale, jnp.float32),
            jnp.ones((2 * model_width,), jnp.float32),
        ]
    )
    onehot = onehot_table()
    region_win = to_windows(regions)
    region_mask = jnp.where(region_win[:, :, None] == region_win[:, None, :], 0.0, -100.0).astype(
        jnp.float32
    )
    window_count = region_win.shape[0]
    tokens = window_count * WIN * WIN

    def score_bias(layer_num):
        table_rows = jnp.dot(onehot, rel_table[layer_num].astype(jnp.float32), precision=highest)
        bias_full = table_rows.T.reshape(head_count, WIN * WIN, WIN * WIN)[None]
        if layer_num % 2 == 1:
            bias_full = bias_full + region_mask[:, None]
        return bias_full

    def heads_of(flat):
        return flat.reshape(window_count, WIN * WIN, head_count, head_dim)

    gathered = []
    for layer_num in range(layer_count):
        own = pack_local(
            w_qkv[layer_num], w_proj[layer_num], w_fc1[layer_num], w_fc2[layer_num],
            norm_gains[layer_num], norm_shifts[layer_num], branch_biases[layer_num],
            fc1_bias[layer_num],
        )
        packed = lax.all_gather(own, "shard", axis=0, tiled=False)
        gathered.append(
            unpack_gathered(packed, w_qkv[layer_num], w_fc1[layer_num], w_fc2[layer_num])
        )
    residual = images.astype(jnp.float32)
    saved_acts = []
    for layer_num in range(layer_count):
        shifted = layer_num % 2 == 1
        attn_w, mlp_w = gathered[layer_num]
        wqkv, wproj, gains, shifts, biases = attn_w
        gains = gains.astype(jnp.float32)
        shifts = shifts.astype(jnp.float32)
        biases = biases.astype(jnp.float32)
        normed = layer_norm(residual, gains[0], shifts[0]).astype(jnp.bfloat16)
        if shifted:
            normed = jnp.roll(normed, (-SHIFT, -SHIFT), axis=(1, 2))
        window_rows = to_windows(normed).reshape(tokens, model_width)
        projected = jnp.dot(window_rows, wqkv, preferred_element_type=jnp.float32)
        queries = heads_of(
            ((projected[:, :model_width] + biases[0]) * query_scale).astype(jnp.bfloat16)
        )
        key_rows = heads_of(projected[:, model_width : 2 * model_width].astype(jnp.bfloat16))
        values = heads_of((projected[:, 2 * model_width :] + biases[1]).astype(jnp.bfloat16))
        scores = jnp.einsum(
            "nqhd,nkhd->nhqk", queries, key_rows, preferred_element_type=jnp.float32
        ) + score_bias(layer_num)
        row_max = jnp.max(scores, axis=-1, keepdims=True)
        log_total = row_max + jnp.log(jnp.sum(jnp.exp(scores - row_max), axis=-1, keepdims=True))
        attn_probs = jnp.exp(scores - log_total).astype(jnp.bfloat16)
        mixed_rows = jnp.einsum(
            "nhqk,nkhd->nqhd", attn_probs, values, preferred_element_type=jnp.float32
        )
        mixed_rows = mixed_rows.reshape(tokens, model_width).astype(jnp.bfloat16)
        branch = jnp.dot(mixed_rows, wproj, preferred_element_type=jnp.float32) + biases[2]
        branch = from_windows(branch.reshape(window_count, WIN * WIN, model_width), image_count)
        if shifted:
            branch = jnp.roll(branch, (SHIFT, SHIFT), axis=(1, 2))
        middle = residual + branch
        wfirst, wsecond, bias_first = mlp_w
        normed_mlp = (
            layer_norm(middle, gains[1], shifts[1]).astype(jnp.bfloat16).reshape(-1, model_width)
        )
        pre_act = jnp.dot(
            normed_mlp, wfirst, preferred_element_type=jnp.float32
        ) + bias_first.astype(jnp.float32)
        activated = jax.nn.gelu(pre_act, approximate=False).astype(jnp.bfloat16)
        mlp_out = jnp.dot(activated, wsecond, preferred_element_type=jnp.float32) + biases[3]
        saved_acts.append(
            (
                residual,
                window_rows,
                queries,
                key_rows,
                values,
                log_total,
                mixed_rows,
                middle,
                normed_mlp,
                pre_act,
                activated,
            )
        )
        residual = middle + mlp_out.reshape(middle.shape)
    images_out = residual.astype(jnp.bfloat16)
    upstream = cotangent.astype(jnp.float32)
    shares = [None] * layer_count
    table_list = [None] * layer_count
    for layer_num in reversed(range(layer_count)):
        shifted = layer_num % 2 == 1
        (
            residual_in,
            window_rows,
            queries,
            key_rows,
            values,
            log_total,
            mixed_rows,
            middle,
            normed_mlp,
            pre_act,
            activated,
        ) = saved_acts[layer_num]
        (wqkv, wproj, gains, shifts, biases), (wfirst, wsecond, bias_first) = gathered[layer_num]
        gains = gains.astype(jnp.float32)
        shifts = shifts.astype(jnp.float32)
        out_grad = upstream.astype(jnp.bfloat16).reshape(-1, model_width)
        grad_b_second = jnp.sum(out_grad.astype(jnp.float32), axis=0)
        grad_w_second = transposed_times(activated, out_grad)
        act_grad = times_transposed(out_grad, wsecond)
        pre_grad = (act_grad * gelu_slope(pre_act)).astype(jnp.bfloat16)
        grad_b_first = jnp.sum(pre_grad.astype(jnp.float32), axis=0)
        grad_w_first = transposed_times(normed_mlp, pre_grad)
        norm_grad = times_transposed(pre_grad, wfirst).reshape(middle.shape)
        norm_pull = jax.vjp(layer_norm, middle, gains[1], shifts[1])[1]
        middle_part, grad_gain_mlp, grad_shift_mlp = norm_pull(norm_grad)
        middle_grad = upstream + middle_part
        branch_grad = middle_grad
        if shifted:
            branch_grad = jnp.roll(branch_grad, (-SHIFT, -SHIFT), axis=(1, 2))
        branch_rows = to_windows(branch_grad.astype(jnp.bfloat16)).reshape(tokens, model_width)
        grad_b_proj = jnp.sum(branch_rows.astype(jnp.float32), axis=0)
        grad_w_proj = transposed_times(mixed_rows, branch_rows)
        mixed_grad = heads_of(times_transposed(branch_rows, wproj).astype(jnp.bfloat16))
        scores = jnp.einsum(
            "nqhd,nkhd->nhqk", queries, key_rows, preferred_element_type=jnp.float32
        ) + score_bias(layer_num)
        attn_probs = jnp.exp(scores - log_total)
        prob_grad = jnp.einsum(
            "nqhd,nkhd->nhqk", mixed_grad, values, preferred_element_type=jnp.float32
        )
        value_grad = jnp.einsum(
            "nhqk,nqhd->nkhd",
            attn_probs.astype(jnp.bfloat16),
            mixed_grad,
            preferred_element_type=jnp.float32,
        ).astype(jnp.bfloat16)
        score_grad = (
            attn_probs * (prob_grad - jnp.sum(attn_probs * prob_grad, axis=-1, keepdims=True))
        ).astype(jnp.bfloat16)
        table_term = jnp.sum(score_grad.astype(jnp.float32), axis=0).reshape(head_count, -1).T
        table_list[layer_num] = jnp.dot(onehot.T, table_term, precision=highest)
        query_grad = jnp.einsum(
            "nhqk,nkhd->nqhd", score_grad, key_rows, preferred_element_type=jnp.float32
        ).astype(jnp.bfloat16)
        key_grad = jnp.einsum(
            "nhqk,nqhd->nkhd", score_grad, queries, preferred_element_type=jnp.float32
        ).astype(jnp.bfloat16)
        qkv_grad = jnp.concatenate(
            [
                query_grad.reshape(tokens, model_width),
                key_grad.reshape(tokens, model_width),
                value_grad.reshape(tokens, model_width),
            ],
            axis=1,
        )
        grad_w_proj_qkv = transposed_times(window_rows, qkv_grad) * column_scale[None, :]
        grad_b_query = (
            jnp.sum(query_grad.reshape(tokens, model_width).astype(jnp.float32), axis=0)
            * query_scale
        )
        grad_b_value = jnp.sum(value_grad.reshape(tokens, model_width).astype(jnp.float32), axis=0)
        rows_grad = times_transposed(qkv_grad[:, :model_width], wqkv[:, :model_width]) * query_scale
        rows_grad = rows_grad + times_transposed(qkv_grad[:, model_width:], wqkv[:, model_width:])
        normed_grad = from_windows(
            rows_grad.reshape(window_count, WIN * WIN, model_width), image_count
        )
        if shifted:
            normed_grad = jnp.roll(normed_grad, (SHIFT, SHIFT), axis=(1, 2))
        first_pull = jax.vjp(layer_norm, residual_in, gains[0], shifts[0])[1]
        input_part, grad_gain_attn, grad_shift_attn = first_pull(normed_grad)
        upstream = middle_grad + input_part
        gain_grads = jnp.stack([grad_gain_attn, grad_gain_mlp])
        shift_grads = jnp.stack([grad_shift_attn, grad_shift_mlp])
        bias_grads = jnp.stack([grad_b_query, grad_b_value, grad_b_proj, grad_b_second])
        packed_grads = pack_grads(
            grad_w_proj_qkv, grad_w_proj, grad_w_first, grad_w_second,
            gain_grads, shift_grads, bias_grads, grad_b_first, shard_count,
        )
        shares[layer_num] = lax.psum_scatter(
            packed_grads, "shard", scatter_dimension=0, tiled=False
        )
    summed = unpack_shares(rep_sum(jnp.stack(shares), rep_count), w_qkv, w_fc2, fc1_bias)
    table_total = lax.psum(jnp.stack(table_list), ("rep", "shard"))
    return (
        images_out,
        upstream,
        summed[0],
        summed[1],
        summed[2],
        summed[3],
        summed[4],
        summed[5],
        summed[6],
        summed[7],
        table_total,
    )


def solution(mesh):
    return jax.shard_map(
        functools.partial(
            body, rep_count=mesh.shape["rep"], shard_count=mesh.shape["shard"]
        ),
        mesh=mesh,
        in_specs=(
            P(("rep", "shard"), None, None, None),
            P(("rep", "shard"), None, None, None),
            P(("rep", "shard"), None, None),
            P(None, "shard", None),
            P(None, "shard", None),
            P(None, "shard", None),
            P(None, "shard", None),
            P(None, None, "shard"),
            P(None, None, "shard"),
            P(None, None, "shard"),
            P(None, "shard"),
            P(),
        ),
        out_specs=(
            P(("rep", "shard"), None, None, None),
            P(("rep", "shard"), None, None, None),
            P(None, "shard", None),
            P(None, "shard", None),
            P(None, "shard", None),
            P(None, "shard", None),
            P(None, None, "shard"),
            P(None, None, "shard"),
            P(None, None, "shard"),
            P(None, "shard"),
            P(),
        ),
        check_vma=False,
    )
```

```python
import functools

import jax
import jax.numpy as jnp
import numpy as np
from jax import lax
from jax.experimental import pallas as pl
from jax.experimental.pallas import tpu as pltpu
from jax.sharding import PartitionSpec as P

SIDE = 14
WIN = 7
SHIFT = 3
PAD_ROWS = 16
CELLS = WIN * WIN
SLOT = 64
WINDOWS = (SIDE // WIN) ** 2
TOKENS = WINDOWS * SLOT
LANES = 128

eps = 1e-05
highest = lax.Precision.HIGHEST
inv_root_two = 0.7071067811865476
inv_root_two_pi = 0.3989422804014327


def to_windows(grid_data):
    image_count = grid_data.shape[0]
    per_side = SIDE // WIN
    trailing = grid_data.shape[3:]
    blocks = grid_data.reshape((image_count, per_side, WIN, per_side, WIN) + trailing)
    blocks = jnp.swapaxes(blocks, 2, 3)
    return blocks.reshape((image_count * per_side * per_side, WIN * WIN) + trailing)


def from_windows(blocks, image_count):
    per_side = SIDE // WIN
    trailing = blocks.shape[2:]
    grid_data = blocks.reshape((image_count, per_side, per_side, WIN, WIN) + trailing)
    grid_data = jnp.swapaxes(grid_data, 2, 3)
    return grid_data.reshape((image_count, SIDE, SIDE) + trailing)


def pack_local(w_qkv, w_proj, w_fc1, w_fc2, gains, shifts, biases, fc1_bias):
    width = w_proj.shape[1]
    blocks = [w_qkv[:, n * width : (n + 1) * width] for n in range(w_qkv.shape[1] // width)]
    blocks.append(w_proj)
    blocks += [w_fc1[:, n * width : (n + 1) * width] for n in range(w_fc1.shape[1] // width)]
    blocks.append(w_fc2)
    small = jnp.concatenate(
        [gains.reshape(-1), shifts.reshape(-1), biases.reshape(-1), fc1_bias.reshape(-1)]
    )
    small = jnp.pad(small, (0, width - small.shape[0])).reshape(1, width)
    blocks.append(jnp.pad(small, ((0, PAD_ROWS - 1), (0, 0))))
    return jnp.concatenate(blocks, axis=0)


def rep_sum(share, rep_count):
    total = share
    step = 1
    while step < rep_count:
        pairs = [(n, n ^ step) for n in range(rep_count)]
        total = total + lax.ppermute(total, "rep", pairs)
        step *= 2
    return total


def unpack_shares(shares, w_qkv, w_fc2, fc1_bias):
    shares = shares.astype(jnp.float32)
    layer_count, _, width = shares.shape
    rows = w_qkv.shape[1]
    hidden = fc1_bias.shape[1]
    qkv_parts = w_qkv.shape[2] // width
    fc1_parts = (shares.shape[1] - PAD_ROWS - w_fc2.shape[1]) // rows - qkv_parts - 1

    def piece(n):
        return shares[:, n * rows : (n + 1) * rows]

    start = (qkv_parts + 1 + fc1_parts) * rows
    small = shares[:, start + w_fc2.shape[1]]
    return (
        jnp.concatenate([piece(n) for n in range(qkv_parts)], axis=2),
        piece(qkv_parts),
        jnp.concatenate([piece(qkv_parts + 1 + n) for n in range(fc1_parts)], axis=2),
        shares[:, start : start + w_fc2.shape[1]],
        small[:, : 2 * rows].reshape(layer_count, 2, rows),
        small[:, 2 * rows : 4 * rows].reshape(layer_count, 2, rows),
        small[:, 4 * rows : 8 * rows].reshape(layer_count, 4, rows),
        small[:, 8 * rows : 8 * rows + hidden],
    )


def dot(left, right):
    return jnp.dot(left, right, preferred_element_type=jnp.float32)


def dot_nt(left, right):
    return lax.dot_general(
        left, right, (((1,), (1,)), ((), ())), preferred_element_type=jnp.float32
    )


def dot_tn(left, right):
    return lax.dot_general(
        left, right, (((0,), (0,)), ((), ())), preferred_element_type=jnp.float32
    )


def normalise(values):
    row_mean = jnp.mean(values, axis=-1, keepdims=True)
    centred = values - row_mean
    rstd = lax.rsqrt(jnp.mean(centred * centred, axis=-1, keepdims=True) + eps)
    return centred * rstd, rstd


def norm_back(grad, gain, xhat, rstd):
    scaled = grad * gain
    return rstd * (
        scaled
        - jnp.mean(scaled, axis=-1, keepdims=True)
        - xhat * jnp.mean(scaled * xhat, axis=-1, keepdims=True)
    )


def low(values):
    return values.astype(jnp.bfloat16)


class Pieces:
    def __init__(self, ref, width, hidden):
        self.ref = ref
        self.width = width
        self.shards = ref.shape[0]
        self.rows = width // self.shards
        self.hidden = hidden // self.shards
        self.parts = hidden // width
        self.start = (4 + self.parts) * self.rows

    def square(self, n):
        return self.ref[:, n * self.rows : (n + 1) * self.rows, :].reshape(self.width, self.width)

    def second(self, n):
        group = self.shards // self.parts
        return self.ref[
            n * group : (n + 1) * group, self.start : self.start + self.hidden, :
        ].reshape(self.width, self.width)

    def put_square(self, n, value):
        self.ref[:, n * self.rows : (n + 1) * self.rows, :] = low(value).reshape(
            self.shards, self.rows, self.width
        )

    def put_second(self, n, value):
        group = self.shards // self.parts
        self.ref[n * group : (n + 1) * group, self.start : self.start + self.hidden, :] = low(
            value
        ).reshape(group, self.hidden, self.width)


def stack_heads(block, per_group, head_dim):
    lane_head = lax.broadcasted_iota(jnp.int32, block.shape, 1) // head_dim
    zero = jnp.zeros_like(block)
    return jnp.concatenate(
        [jnp.where(lane_head == n, block, zero) for n in range(per_group)], axis=0
    )


def pick_heads(stacked, per_group, head_dim):
    rows = stacked.shape[0] // per_group
    lane_head = lax.broadcasted_iota(jnp.int32, (rows, stacked.shape[1]), 1) // head_dim
    total = stacked[:rows]
    for n in range(1, per_group):
        total = jnp.where(lane_head == n, stacked[n * rows : (n + 1) * rows], total)
    return total


def probs_of(q_stack, key_block, bias_ref, mask_ref, window, group, per_group):
    scores = dot_nt(q_stack, key_block)
    span = per_group * SLOT
    scores = scores + bias_ref[group * span : (group + 1) * span, :]
    if mask_ref is not None:
        region = mask_ref[window]
        scores = scores + jnp.concatenate([region] * per_group, axis=0)
    top = jnp.max(scores, axis=-1, keepdims=True)
    raised = jnp.exp(scores - top)
    return raised / jnp.sum(raised, axis=-1, keepdims=True)


def forward_kernel(shifted, hidden, head_dim, *refs):
    if shifted:
        (r_ref, w_ref, vec_ref, fb_ref, bias_ref, mask_ref, perm_ref, *outs) = refs
    else:
        (r_ref, w_ref, vec_ref, fb_ref, bias_ref, *outs) = refs
        mask_ref = None
    (out_ref, hs_ref, qkv_ref, mixed_ref, mid_ref, h2_ref, slope_ref, act_ref) = outs
    width = r_ref.shape[1]
    weights = Pieces(w_ref, width, hidden)
    scale = head_dim ** (-0.5)
    per_group = LANES // head_dim
    vec = lambda n: vec_ref[n : n + 1, :]
    h = low(normalise(r_ref[...])[0] * vec(0) + vec(2))
    if shifted:
        h = low(dot(perm_ref[...], h))
    hs_ref[...] = h
    qkv_ref[:, :width] = low((dot(h, weights.square(0)) + vec(4)) * scale)
    qkv_ref[:, width : 2 * width] = low(dot(h, weights.square(1)))
    qkv_ref[:, 2 * width :] = low(dot(h, weights.square(2)) + vec(5))

    def window_step(window, carry):
        rows = pl.ds(pl.multiple_of(window * SLOT, SLOT), SLOT)
        for group in range(width // LANES):
            first = group * LANES
            q_stack = stack_heads(qkv_ref[rows, first : first + LANES], per_group, head_dim)
            key_block = qkv_ref[rows, width + first : width + first + LANES]
            value_block = qkv_ref[rows, 2 * width + first : 2 * width + first + LANES]
            probs = low(
                probs_of(q_stack, key_block, bias_ref, mask_ref, window, group, per_group)
            )
            mixed_ref[rows, first : first + LANES] = low(
                pick_heads(dot(probs, value_block), per_group, head_dim)
            )
        return carry

    lax.fori_loop(0, WINDOWS, window_step, 0)
    mixed = mixed_ref[...]
    if shifted:
        mixed = low(dot_tn(perm_ref[...], mixed))
    middle = r_ref[...] + dot(mixed, weights.square(3)) + vec(6)
    mid_ref[...] = middle
    h2 = low(normalise(middle)[0] * vec(1) + vec(3))
    h2_ref[...] = h2
    out_ref[...] = middle + vec(7)
    for part in range(weights.parts):
        cols = slice(part * width, (part + 1) * width)
        pre_act = dot(h2, weights.square(4 + part)) + fb_ref[:, cols]
        half_cdf = 0.5 * (1.0 + lax.erf(pre_act * inv_root_two))
        act = low(pre_act * half_cdf)
        act_ref[:, cols] = act
        slope_ref[:, cols] = half_cdf + pre_act * inv_root_two_pi * jnp.exp(
            -0.5 * pre_act * pre_act
        )
        out_ref[...] += dot(act, weights.second(part))


def backward_kernel(shifted, hidden, head_dim, *refs):
    if shifted:
        (g_ref, w_ref, vec_ref, bias_ref, mask_ref, perm_ref, *rest) = refs
    else:
        (g_ref, w_ref, vec_ref, bias_ref, *rest) = refs
        mask_ref = None
    (r_ref, hs_ref, qkv_ref, mixed_ref, mid_ref, h2_ref, slope_ref, act_ref, *rest) = rest
    (up_ref, gw_ref, small_ref, ds_ref, dmix_ref, dqkv_ref) = rest
    width = r_ref.shape[1]
    weights = Pieces(w_ref, width, hidden)
    grads = Pieces(gw_ref, width, hidden)
    scale = head_dim ** (-0.5)
    per_group = LANES // head_dim
    vec = lambda n: vec_ref[n : n + 1, :]

    def put_sum(n, values):
        small_ref[n : n + 1, :] = jnp.sum(values.astype(jnp.float32), axis=0, keepdims=True)

    small_ref[...] = jnp.zeros_like(small_ref)
    first_spare = grads.start + grads.hidden
    gw_ref[:, first_spare:, :] = jnp.zeros(
        (grads.shards, gw_ref.shape[1] - first_spare, width), jnp.bfloat16
    )
    upstream = g_ref[...]
    out_grad = low(upstream)
    put_sum(7, out_grad)
    h2 = h2_ref[...]
    norm_grad = jnp.zeros(upstream.shape, jnp.float32)
    for part in range(weights.parts):
        cols = slice(part * width, (part + 1) * width)
        grads.put_second(part, dot_tn(act_ref[:, cols], out_grad))
        pre_grad = low(dot_nt(out_grad, weights.second(part)) * slope_ref[:, cols])
        put_sum(8 + part, pre_grad)
        grads.put_square(4 + part, dot_tn(h2, pre_grad))
        norm_grad = norm_grad + dot_nt(pre_grad, weights.square(4 + part))
    xhat, rstd = normalise(mid_ref[...])
    put_sum(1, norm_grad * xhat)
    put_sum(3, norm_grad)
    middle_grad = upstream + norm_back(norm_grad, vec(1), xhat, rstd)
    branch_grad = low(middle_grad)
    if shifted:
        branch_grad = low(dot(perm_ref[...], branch_grad))
    put_sum(6, branch_grad)
    grads.put_square(3, dot_tn(mixed_ref[...], branch_grad))
    dmix_ref[...] = low(dot_nt(branch_grad, weights.square(3)))
    ds_ref[...] = jnp.zeros_like(ds_ref)

    def window_step(window, carry):
        rows = pl.ds(pl.multiple_of(window * SLOT, SLOT), SLOT)
        for group in range(width // LANES):
            first = group * LANES
            span = per_group * SLOT
            q_stack = stack_heads(qkv_ref[rows, first : first + LANES], per_group, head_dim)
            d_stack = stack_heads(dmix_ref[rows, first : first + LANES], per_group, head_dim)
            key_block = qkv_ref[rows, width + first : width + first + LANES]
            value_block = qkv_ref[rows, 2 * width + first : 2 * width + first + LANES]
            probs = probs_of(q_stack, key_block, bias_ref, mask_ref, window, group, per_group)
            prob_grad = dot_nt(d_stack, value_block)
            value_grad = dot_tn(low(probs), d_stack)
            score_grad = low(
                probs * (prob_grad - jnp.sum(probs * prob_grad, axis=-1, keepdims=True))
            )
            ds_ref[group * span : (group + 1) * span, :] += score_grad.astype(jnp.float32)
            dqkv_ref[rows, first : first + LANES] = low(
                pick_heads(dot(score_grad, key_block), per_group, head_dim)
            )
            dqkv_ref[rows, width + first : width + first + LANES] = low(
                dot_tn(score_grad, q_stack)
            )
            dqkv_ref[rows, 2 * width + first : 2 * width + first + LANES] = low(value_grad)
        return carry

    lax.fori_loop(0, WINDOWS, window_step, 0)
    hs = hs_ref[...]
    rows_grad = jnp.zeros(upstream.shape, jnp.float32)
    for part in range(3):
        piece = dqkv_ref[:, part * width : (part + 1) * width]
        weight_grad = dot_tn(hs, piece)
        factor = scale if part == 0 else 1.0
        grads.put_square(part, weight_grad * factor)
        if part == 0:
            put_sum(4, piece.astype(jnp.float32) * scale)
        if part == 2:
            put_sum(5, piece)
        if shifted:
            piece = low(dot_tn(perm_ref[...], piece))
        rows_grad = rows_grad + dot_nt(piece, weights.square(part)) * factor
    xhat, rstd = normalise(r_ref[...])
    put_sum(0, rows_grad * xhat)
    put_sum(2, rows_grad)
    up_ref[...] = middle_grad + norm_back(rows_grad, vec(0), xhat, rstd)


def call_kernel(kernel, outs, scratch, args, flops, name):
    vmem = pl.BlockSpec(memory_space=pltpu.VMEM)
    return pl.pallas_call(
        kernel,
        out_shape=[jax.ShapeDtypeStruct(shape, kind) for shape, kind in outs],
        in_specs=[vmem] * len(args),
        out_specs=[vmem] * len(outs),
        scratch_shapes=[pltpu.VMEM(shape, kind) for shape, kind in scratch],
        compiler_params=pltpu.CompilerParams(vmem_limit_bytes=58 * 1024 * 1024),
        cost_estimate=pl.CostEstimate(flops=flops, bytes_accessed=20_000_000, transcendentals=0),
        name=name,
    )(*args)


def table_onehot():
    cell_row = np.arange(CELLS) // WIN
    cell_col = np.arange(CELLS) % WIN
    side = 2 * WIN - 1
    rel = (cell_row[:, None] - cell_row[None, :] + WIN - 1) * side + (
        cell_col[:, None] - cell_col[None, :] + WIN - 1
    )
    padded = np.full((SLOT, SLOT), -1)
    padded[:CELLS, :CELLS] = rel
    return jnp.asarray(padded.reshape(-1), jnp.int32)[:, None] == jnp.arange(side * side)[None, :]


def shift_matrix():
    cell = np.arange(SIDE * SIDE).reshape(SIDE, SIDE)

    def slots(grid):
        blocks = grid.reshape(SIDE // WIN, WIN, SIDE // WIN, WIN).swapaxes(1, 2)
        blocks = blocks.reshape(WINDOWS, CELLS)
        return np.pad(blocks, ((0, 0), (0, SLOT - CELLS)), constant_values=-1).reshape(-1)

    plain, moved = slots(cell), slots(np.roll(cell, (-SHIFT, -SHIFT), axis=(0, 1)))
    plain = np.where(plain < 0, -2, plain)
    return low(jnp.asarray(moved, jnp.int32)[:, None] == jnp.asarray(plain, jnp.int32)[None, :])


def to_slots(grid):
    blocks = to_windows(grid)
    return jnp.pad(blocks, ((0, 0), (0, SLOT - CELLS), (0, 0))).reshape(TOKENS, grid.shape[3])


def from_slots(rows):
    return from_windows(rows.reshape(WINDOWS, SLOT, -1)[:, :CELLS], 1)


def body(
    images, cotangent, regions, w_qkv, w_proj, w_fc1, w_fc2,
    norm_gains, norm_shifts, branch_biases, fc1_bias, rel_table,
    rep_count, shard_count,
):
    layer_count = w_qkv.shape[0]
    width = w_proj.shape[2]
    head_count = rel_table.shape[2]
    head_dim = width // head_count
    hidden = w_fc1.shape[2]
    rows, hidden_own = w_qkv.shape[1], w_fc2.shape[1]
    gathered = []
    for n in range(layer_count):
        own = pack_local(
            w_qkv[n], w_proj[n], w_fc1[n], w_fc2[n],
            norm_gains[n], norm_shifts[n], branch_biases[n], fc1_bias[n],
        )
        gathered.append(lax.all_gather(own, "shard", axis=0, tiled=False))
    onehot = table_onehot()
    spare = jnp.where(jnp.arange(SLOT) < CELLS, 0.0, -1e30).astype(jnp.float32)
    score_bias = lax.dot_general(
        rel_table, low(onehot), (((1,), (1,)), ((), ())), preferred_element_type=jnp.float32
    )
    score_bias = score_bias.reshape(layer_count, head_count * SLOT, SLOT) + spare
    region_win = jnp.pad(to_windows(regions), ((0, 0), (0, SLOT - CELLS)), constant_values=-1)
    region_mask = jnp.where(region_win[:, :, None] == region_win[:, None, :], 0.0, -100.0).astype(
        jnp.float32
    )
    perm = shift_matrix()
    f32, bf16 = jnp.float32, jnp.bfloat16
    residual = to_slots(images).astype(f32)
    flops = 2 * TOKENS * (4 * width + 2 * hidden) * width
    saved = []
    for n in range(layer_count):
        shifted = n % 2 == 1
        packed = gathered[n]
        small = packed[:, packed.shape[1] - PAD_ROWS]
        vec = small[:, : 8 * rows].reshape(shard_count, 8, rows)
        vec = jnp.swapaxes(vec, 0, 1).reshape(8, width).astype(f32)
        fb = small[:, 8 * rows : 8 * rows + hidden_own].reshape(1, hidden).astype(f32)
        extra = [region_mask, perm] if shifted else []
        out, *acts = call_kernel(
            functools.partial(forward_kernel, shifted, hidden, head_dim),
            [
                ((TOKENS, width), f32), ((TOKENS, width), bf16), ((TOKENS, 3 * width), bf16),
                ((TOKENS, width), bf16), ((TOKENS, width), f32), ((TOKENS, width), bf16),
                ((TOKENS, hidden), f32), ((TOKENS, hidden), bf16),
            ],
            [],
            [residual, packed, vec, fb, score_bias[n], *extra],
            flops,
            "block_forward",
        )
        saved.append((packed, vec, extra, [residual, *acts]))
        residual = out
    images_out = from_slots(low(residual))
    upstream = to_slots(cotangent).astype(f32)
    shares = [None] * layer_count
    tables = [None] * layer_count
    for n in reversed(range(layer_count)):
        packed, vec, extra, acts = saved[n]
        upstream, weight_grads, small, tables[n] = call_kernel(
            functools.partial(backward_kernel, n % 2 == 1, hidden, head_dim),
            [
                ((TOKENS, width), f32), (packed.shape, bf16),
                ((8 + hidden // width + 4, width), f32), ((head_count * SLOT, SLOT), f32),
            ],
            [((TOKENS, width), bf16), ((TOKENS, 3 * width), bf16)],
            [upstream, packed, vec, score_bias[n], *extra, *acts],
            2 * flops,
            "block_backward",
        )
        vec_part = jnp.swapaxes(small[:8].reshape(8, shard_count, rows), 0, 1)
        fb_part = small[8 : 8 + hidden // width].reshape(shard_count, hidden_own)
        small = low(jnp.concatenate([vec_part.reshape(shard_count, -1), fb_part], axis=1))
        weight_grads = lax.dynamic_update_slice(
            weight_grads, small[:, None], (0, packed.shape[1] - PAD_ROWS, 0)
        )
        shares[n] = lax.psum_scatter(weight_grads, "shard", scatter_dimension=0, tiled=False)
    summed = unpack_shares(rep_sum(jnp.stack(shares), rep_count), w_qkv, w_fc2, fc1_bias)
    table_terms = jnp.stack(tables).reshape(layer_count, head_count, SLOT * SLOT)
    table_grad = lax.dot_general(
        onehot.astype(f32), table_terms, (((0,), (2,)), ((), ())), precision=highest
    )
    table_total = lax.psum(jnp.swapaxes(table_grad, 0, 1), ("rep", "shard"))
    return (images_out, from_slots(upstream), *summed, table_total)


def solution(mesh):
    return jax.shard_map(
        functools.partial(
            body, rep_count=mesh.shape["rep"], shard_count=mesh.shape["shard"]
        ),
        mesh=mesh,
        in_specs=(
            P(("rep", "shard"), None, None, None),
            P(("rep", "shard"), None, None, None),
            P(("rep", "shard"), None, None),
            P(None, "shard", None),
            P(None, "shard", None),
            P(None, "shard", None),
            P(None, "shard", None),
            P(None, None, "shard"),
            P(None, None, "shard"),
            P(None, None, "shard"),
            P(None, "shard"),
            P(),
        ),
        out_specs=(
            P(("rep", "shard"), None, None, None),
            P(("rep", "shard"), None, None, None),
            P(None, "shard", None),
            P(None, "shard", None),
            P(None, "shard", None),
            P(None, "shard", None),
            P(None, None, "shard"),
            P(None, None, "shard"),
            P(None, None, "shard"),
            P(None, "shard"),
            P(),
        ),
        check_vma=False,
    )
```

```python
import functools

import jax
import jax.numpy as jnp
import numpy as np
from jax import lax
from jax.experimental import pallas as pl
from jax.experimental.pallas import tpu as pltpu
from jax.sharding import PartitionSpec as P

SIDE = 14
WIN = 7
SHIFT = 3
PAD_ROWS = 16
CELLS = WIN * WIN
SLOT = 64
WINDOWS = (SIDE // WIN) ** 2
TOKENS = WINDOWS * SLOT
LANES = 128

eps = 1e-05
highest = lax.Precision.HIGHEST
inv_root_two = 0.7071067811865476
inv_root_two_pi = 0.3989422804014327


def to_windows(grid_data):
    image_count = grid_data.shape[0]
    per_side = SIDE // WIN
    trailing = grid_data.shape[3:]
    blocks = grid_data.reshape((image_count, per_side, WIN, per_side, WIN) + trailing)
    blocks = jnp.swapaxes(blocks, 2, 3)
    return blocks.reshape((image_count * per_side * per_side, WIN * WIN) + trailing)


def from_windows(blocks, image_count):
    per_side = SIDE // WIN
    trailing = blocks.shape[2:]
    grid_data = blocks.reshape((image_count, per_side, per_side, WIN, WIN) + trailing)
    grid_data = jnp.swapaxes(grid_data, 2, 3)
    return grid_data.reshape((image_count, SIDE, SIDE) + trailing)


def vector_tile(parts, width):
    parts = [jnp.pad(part, ((0, width - part.shape[0]),)) for part in parts]
    return jnp.pad(jnp.stack(parts), ((0, PAD_ROWS - len(parts)), (0, 0)))


def pack_local(w_qkv, w_proj, w_fc1, w_fc2, gains, shifts, biases, fc1_bias):
    width = w_proj.shape[2]
    blocks, smalls = [], []
    for n in range(w_qkv.shape[0]):
        for block in (w_qkv[n], w_proj[n], w_fc1[n], w_fc2[n]):
            parts = block.shape[1] // width
            blocks += [block[:, m * width : (m + 1) * width] for m in range(parts)]
        vectors = (gains[n], shifts[n], biases[n], fc1_bias[n])
        smalls.append(jnp.concatenate([vector.reshape(-1) for vector in vectors]))
    return jnp.concatenate([*blocks, vector_tile(smalls, width)], axis=0)


def rep_sum(share, rep_count):
    total = share.astype(jnp.float32)
    step = 1
    while step < rep_count:
        pairs = [(n, n ^ step) for n in range(rep_count)]
        sent = low(total)
        arrived = lax.ppermute(sent, "rep", pairs)
        total = sent.astype(jnp.float32) + arrived.astype(jnp.float32)
        step *= 2
    return total


def unpack_shares(shares, w_qkv, w_fc2, fc1_bias):
    layer_count, rows = w_qkv.shape[:2]
    width = shares.shape[1]
    hidden_own = fc1_bias.shape[1]
    blocks = shares[:-PAD_ROWS].reshape(layer_count, -1, width)
    qkv_parts = w_qkv.shape[2] // width
    fc1_parts = (blocks.shape[1] - w_fc2.shape[1]) // rows - qkv_parts - 1

    def piece(n):
        return blocks[:, n * rows : (n + 1) * rows]

    start = (qkv_parts + 1 + fc1_parts) * rows
    small = shares[blocks.shape[0] * blocks.shape[1] :][:layer_count]
    return (
        jnp.concatenate([piece(n) for n in range(qkv_parts)], axis=2),
        piece(qkv_parts),
        jnp.concatenate([piece(qkv_parts + 1 + n) for n in range(fc1_parts)], axis=2),
        blocks[:, start:],
        small[:, : 2 * rows].reshape(layer_count, 2, rows),
        small[:, 2 * rows : 4 * rows].reshape(layer_count, 2, rows),
        small[:, 4 * rows : 8 * rows].reshape(layer_count, 4, rows),
        small[:, 8 * rows : 8 * rows + hidden_own],
    )


def dot(left, right):
    return jnp.dot(left, right, preferred_element_type=jnp.float32)


def dot_nt(left, right):
    return lax.dot_general(
        left, right, (((1,), (1,)), ((), ())), preferred_element_type=jnp.float32
    )


def dot_tn(left, right):
    return lax.dot_general(
        left, right, (((0,), (0,)), ((), ())), preferred_element_type=jnp.float32
    )


def normalise(values):
    row_mean = jnp.mean(values, axis=-1, keepdims=True)
    centred = values - row_mean
    rstd = lax.rsqrt(jnp.mean(centred * centred, axis=-1, keepdims=True) + eps)
    return centred * rstd, rstd


def norm_back(grad, gain, xhat, rstd):
    scaled = grad * gain
    return rstd * (
        scaled
        - jnp.mean(scaled, axis=-1, keepdims=True)
        - xhat * jnp.mean(scaled * xhat, axis=-1, keepdims=True)
    )


def low(values):
    return values.astype(jnp.bfloat16)


class Pieces:
    def __init__(self, ref, width, hidden, layer):
        self.ref = ref
        self.width = width
        self.shards = ref.shape[0]
        self.rows = width // self.shards
        self.hidden = hidden // self.shards
        self.parts = hidden // width
        self.base = layer * ((4 + self.parts) * self.rows + self.hidden)
        self.start = self.base + (4 + self.parts) * self.rows

    def span(self, n):
        first = self.base + n * self.rows
        return slice(first, first + self.rows)

    def square(self, n):
        return self.ref[:, self.span(n), :].reshape(self.width, self.width)

    def second(self, n):
        group = self.shards // self.parts
        return self.ref[
            n * group : (n + 1) * group, self.start : self.start + self.hidden, :
        ].reshape(self.width, self.width)

    def put_square(self, n, value):
        self.ref[:, self.span(n), :] = low(value).reshape(
            self.shards, self.rows, self.width
        )

    def put_second(self, n, value):
        group = self.shards // self.parts
        self.ref[n * group : (n + 1) * group, self.start : self.start + self.hidden, :] = low(
            value
        ).reshape(group, self.hidden, self.width)


def stack_heads(block, per_group, head_dim):
    lane_head = lax.broadcasted_iota(jnp.int32, block.shape, 1) // head_dim
    zero = jnp.zeros_like(block)
    return jnp.concatenate(
        [jnp.where(lane_head == n, block, zero) for n in range(per_group)], axis=0
    )


def pick_heads(stacked, per_group, head_dim):
    rows = stacked.shape[0] // per_group
    lane_head = lax.broadcasted_iota(jnp.int32, (rows, stacked.shape[1]), 1) // head_dim
    total = stacked[:rows]
    for n in range(1, per_group):
        total = jnp.where(lane_head == n, stacked[n * rows : (n + 1) * rows], total)
    return total


def probs_of(q_stack, key_block, bias_ref, mask_ref, window, group, per_group):
    scores = dot_nt(q_stack, key_block)
    span = per_group * SLOT
    scores = scores + bias_ref[group * span : (group + 1) * span, :]
    if mask_ref is not None:
        region = mask_ref[window]
        scores = scores + jnp.concatenate([region] * per_group, axis=0)
    top = jnp.max(scores, axis=-1, keepdims=True)
    raised = jnp.exp(scores - top)
    return raised / jnp.sum(raised, axis=-1, keepdims=True)


def forward_block(layer, hidden, head_dim, r_ref, out_ref, ins, acts):
    shifted = layer % 2 == 1
    (w_ref, vec_ref, fb_ref, bias_ref, mask_ref, perm_ref) = ins
    vec_ref, fb_ref, bias_ref = vec_ref.at[layer], fb_ref.at[layer], bias_ref.at[layer]
    mask_ref = mask_ref if shifted else None
    (hs_ref, qkv_ref, mixed_ref, mid_ref, h2_ref, slope_ref, act_ref) = (
        act.at[layer] for act in acts
    )
    width = r_ref.shape[1]
    weights = Pieces(w_ref, width, hidden, layer)
    scale = head_dim ** (-0.5)
    per_group = LANES // head_dim
    vec = lambda n: vec_ref[n : n + 1, :]
    h = low(normalise(r_ref[...])[0] * vec(0) + vec(2))
    if shifted:
        h = low(dot(perm_ref[...], h))
    hs_ref[...] = h
    qkv_ref[:, :width] = low((dot(h, weights.square(0)) + vec(4)) * scale)
    qkv_ref[:, width : 2 * width] = low(dot(h, weights.square(1)))
    qkv_ref[:, 2 * width :] = low(dot(h, weights.square(2)) + vec(5))

    def window_step(window, carry):
        rows = pl.ds(pl.multiple_of(window * SLOT, SLOT), SLOT)
        for group in range(width // LANES):
            first = group * LANES
            q_stack = stack_heads(qkv_ref[rows, first : first + LANES], per_group, head_dim)
            key_block = qkv_ref[rows, width + first : width + first + LANES]
            value_block = qkv_ref[rows, 2 * width + first : 2 * width + first + LANES]
            probs = low(
                probs_of(q_stack, key_block, bias_ref, mask_ref, window, group, per_group)
            )
            mixed_ref[rows, first : first + LANES] = low(
                pick_heads(dot(probs, value_block), per_group, head_dim)
            )
        return carry

    lax.fori_loop(0, WINDOWS, window_step, 0)
    mixed = mixed_ref[...]
    if shifted:
        mixed = low(dot_tn(perm_ref[...], mixed))
    middle = r_ref[...] + dot(mixed, weights.square(3)) + vec(6)
    mid_ref[...] = middle
    h2 = low(normalise(middle)[0] * vec(1) + vec(3))
    h2_ref[...] = h2
    out_ref[...] = middle + vec(7)
    for part in range(weights.parts):
        cols = slice(part * width, (part + 1) * width)
        pre_act = dot(h2, weights.square(4 + part)) + fb_ref[:, cols]
        half_cdf = 0.5 * (1.0 + lax.erf(pre_act * inv_root_two))
        act = low(pre_act * half_cdf)
        act_ref[:, cols] = act
        slope_ref[:, cols] = half_cdf + pre_act * inv_root_two_pi * jnp.exp(
            -0.5 * pre_act * pre_act
        )
        out_ref[...] += dot(act, weights.second(part))


def backward_block(layer, hidden, head_dim, r_ref, g_ref, up_ref, ins, acts, gw_ref, rest):
    shifted = layer % 2 == 1
    (w_ref, vec_ref, _, bias_ref, mask_ref, perm_ref) = ins
    vec_ref, bias_ref = vec_ref.at[layer], bias_ref.at[layer]
    mask_ref = mask_ref if shifted else None
    (hs_ref, qkv_ref, mixed_ref, mid_ref, h2_ref, slope_ref, act_ref) = (
        act.at[layer] for act in acts
    )
    (small_ref, ds_ref, dmix_ref, dqkv_ref) = rest
    small_ref, ds_ref = small_ref.at[layer], ds_ref.at[layer]
    width = r_ref.shape[1]
    weights = Pieces(w_ref, width, hidden, layer)
    grads = Pieces(gw_ref, width, hidden, layer)
    scale = head_dim ** (-0.5)
    per_group = LANES // head_dim
    vec = lambda n: vec_ref[n : n + 1, :]

    def put_sum(n, values):
        small_ref[n : n + 1, :] = jnp.sum(values.astype(jnp.float32), axis=0, keepdims=True)

    small_ref[...] = jnp.zeros_like(small_ref)
    upstream = g_ref[...]
    out_grad = low(upstream)
    put_sum(7, out_grad)
    h2 = h2_ref[...]
    norm_grad = jnp.zeros(upstream.shape, jnp.float32)
    for part in range(weights.parts):
        cols = slice(part * width, (part + 1) * width)
        grads.put_second(part, dot_tn(act_ref[:, cols], out_grad))
        pre_grad = low(dot_nt(out_grad, weights.second(part)) * slope_ref[:, cols])
        put_sum(8 + part, pre_grad)
        grads.put_square(4 + part, dot_tn(h2, pre_grad))
        norm_grad = norm_grad + dot_nt(pre_grad, weights.square(4 + part))
    xhat, rstd = normalise(mid_ref[...])
    put_sum(1, norm_grad * xhat)
    put_sum(3, norm_grad)
    middle_grad = upstream + norm_back(norm_grad, vec(1), xhat, rstd)
    branch_grad = low(middle_grad)
    if shifted:
        branch_grad = low(dot(perm_ref[...], branch_grad))
    put_sum(6, branch_grad)
    grads.put_square(3, dot_tn(mixed_ref[...], branch_grad))
    dmix_ref[...] = low(dot_nt(branch_grad, weights.square(3)))
    ds_ref[...] = jnp.zeros_like(ds_ref)

    def window_step(window, carry):
        rows = pl.ds(pl.multiple_of(window * SLOT, SLOT), SLOT)
        for group in range(width // LANES):
            first = group * LANES
            span = per_group * SLOT
            q_stack = stack_heads(qkv_ref[rows, first : first + LANES], per_group, head_dim)
            d_stack = stack_heads(dmix_ref[rows, first : first + LANES], per_group, head_dim)
            key_block = qkv_ref[rows, width + first : width + first + LANES]
            value_block = qkv_ref[rows, 2 * width + first : 2 * width + first + LANES]
            probs = probs_of(q_stack, key_block, bias_ref, mask_ref, window, group, per_group)
            prob_grad = dot_nt(d_stack, value_block)
            value_grad = dot_tn(low(probs), d_stack)
            score_grad = low(
                probs * (prob_grad - jnp.sum(probs * prob_grad, axis=-1, keepdims=True))
            )
            ds_ref[group * span : (group + 1) * span, :] += score_grad.astype(jnp.float32)
            dqkv_ref[rows, first : first + LANES] = low(
                pick_heads(dot(score_grad, key_block), per_group, head_dim)
            )
            dqkv_ref[rows, width + first : width + first + LANES] = low(
                dot_tn(score_grad, q_stack)
            )
            dqkv_ref[rows, 2 * width + first : 2 * width + first + LANES] = low(value_grad)
        return carry

    lax.fori_loop(0, WINDOWS, window_step, 0)
    hs = hs_ref[...]
    rows_grad = jnp.zeros(upstream.shape, jnp.float32)
    for part in range(3):
        piece = dqkv_ref[:, part * width : (part + 1) * width]
        weight_grad = dot_tn(hs, piece)
        factor = scale if part == 0 else 1.0
        grads.put_square(part, weight_grad * factor)
        if part == 0:
            put_sum(4, piece.astype(jnp.float32) * scale)
        if part == 2:
            put_sum(5, piece)
        if shifted:
            piece = low(dot_tn(perm_ref[...], piece))
        rows_grad = rows_grad + dot_nt(piece, weights.square(part)) * factor
    xhat, rstd = normalise(r_ref[...])
    put_sum(0, rows_grad * xhat)
    put_sum(2, rows_grad)
    up_ref[...] = middle_grad + norm_back(rows_grad, vec(0), xhat, rstd)


def step_kernel(layer_count, hidden, head_dim, *refs):
    (x_ref, ct_ref, *ins) = refs[:8]
    (out_ref, up_ref, gw_ref, small_ref, ds_ref) = refs[8:13]
    (res_ref, grad_ref, *acts, dmix_ref, dqkv_ref) = refs[13:]
    res_ref[0] = x_ref[...].astype(jnp.float32)
    for layer in range(layer_count):
        forward_block(
            layer, hidden, head_dim, res_ref.at[layer], res_ref.at[layer + 1], ins, acts
        )
    out_ref[...] = low(res_ref[layer_count])
    grad_ref[...] = ct_ref[...].astype(jnp.float32)
    gw_ref[:, gw_ref.shape[1] - PAD_ROWS :, :] = jnp.zeros(
        (gw_ref.shape[0], PAD_ROWS, gw_ref.shape[2]), jnp.bfloat16
    )
    rest = (small_ref, ds_ref, dmix_ref, dqkv_ref)
    for layer in reversed(range(layer_count)):
        target = grad_ref if layer else up_ref
        backward_block(
            layer, hidden, head_dim, res_ref.at[layer], grad_ref, target, ins, acts, gw_ref, rest
        )


def call_kernel(kernel, outs, scratch, args, flops, name):
    vmem = pl.BlockSpec(memory_space=pltpu.VMEM)
    return pl.pallas_call(
        kernel,
        out_shape=[jax.ShapeDtypeStruct(shape, kind) for shape, kind in outs],
        in_specs=[vmem] * len(args),
        out_specs=[vmem] * len(outs),
        scratch_shapes=[pltpu.VMEM(shape, kind) for shape, kind in scratch],
        compiler_params=pltpu.CompilerParams(vmem_limit_bytes=58 * 1024 * 1024),
        cost_estimate=pl.CostEstimate(flops=flops, bytes_accessed=20_000_000, transcendentals=0),
        name=name,
    )(*args)


def table_onehot():
    cell_row = np.arange(CELLS) // WIN
    cell_col = np.arange(CELLS) % WIN
    side = 2 * WIN - 1
    rel = (cell_row[:, None] - cell_row[None, :] + WIN - 1) * side + (
        cell_col[:, None] - cell_col[None, :] + WIN - 1
    )
    padded = np.full((SLOT, SLOT), -1)
    padded[:CELLS, :CELLS] = rel
    return jnp.asarray(padded.reshape(-1), jnp.int32)[:, None] == jnp.arange(side * side)[None, :]


def shift_matrix():
    cell = np.arange(SIDE * SIDE).reshape(SIDE, SIDE)

    def slots(grid):
        blocks = grid.reshape(SIDE // WIN, WIN, SIDE // WIN, WIN).swapaxes(1, 2)
        blocks = blocks.reshape(WINDOWS, CELLS)
        return np.pad(blocks, ((0, 0), (0, SLOT - CELLS)), constant_values=-1).reshape(-1)

    plain, moved = slots(cell), slots(np.roll(cell, (-SHIFT, -SHIFT), axis=(0, 1)))
    plain = np.where(plain < 0, -2, plain)
    return low(jnp.asarray(moved, jnp.int32)[:, None] == jnp.asarray(plain, jnp.int32)[None, :])


def to_slots(grid):
    blocks = to_windows(grid)
    return jnp.pad(blocks, ((0, 0), (0, SLOT - CELLS), (0, 0))).reshape(TOKENS, grid.shape[3])


def from_slots(rows):
    return from_windows(rows.reshape(WINDOWS, SLOT, -1)[:, :CELLS], 1)


def body(
    images, cotangent, regions, w_qkv, w_proj, w_fc1, w_fc2,
    norm_gains, norm_shifts, branch_biases, fc1_bias, rel_table,
    rep_count, shard_count,
):
    layer_count = w_qkv.shape[0]
    width = w_proj.shape[2]
    head_count = rel_table.shape[2]
    head_dim = width // head_count
    hidden = w_fc1.shape[2]
    rows, hidden_own = w_qkv.shape[1], w_fc2.shape[1]
    own = pack_local(
        w_qkv, w_proj, w_fc1, w_fc2, norm_gains, norm_shifts, branch_biases, fc1_bias
    )
    packed = lax.all_gather(own, "shard", axis=0, tiled=False)
    onehot = table_onehot()
    spare = jnp.where(jnp.arange(SLOT) < CELLS, 0.0, -1e30).astype(jnp.float32)
    score_bias = lax.dot_general(
        rel_table, low(onehot), (((1,), (1,)), ((), ())), preferred_element_type=jnp.float32
    )
    score_bias = score_bias.reshape(layer_count, head_count * SLOT, SLOT) + spare
    region_win = jnp.pad(to_windows(regions), ((0, 0), (0, SLOT - CELLS)), constant_values=-1)
    region_mask = jnp.where(region_win[:, :, None] == region_win[:, None, :], 0.0, -100.0).astype(
        jnp.float32
    )
    perm = shift_matrix()
    f32, bf16 = jnp.float32, jnp.bfloat16
    flops = 6 * layer_count * TOKENS * (4 * width + 2 * hidden) * width
    small = packed[:, packed.shape[1] - PAD_ROWS :][:, :layer_count]
    vec = small[:, :, : 8 * rows].reshape(shard_count, layer_count, 8, rows)
    vec = vec.transpose(1, 2, 0, 3).reshape(layer_count, 8, width).astype(f32)
    fb = small[:, :, 8 * rows : 8 * rows + hidden_own]
    fb = jnp.swapaxes(fb, 0, 1).reshape(layer_count, 1, hidden).astype(f32)

    def kept(columns, kind):
        return ((layer_count, TOKENS, columns), kind)

    out, upstream, weight_grads, small, tables = call_kernel(
        functools.partial(step_kernel, layer_count, hidden, head_dim),
        [
            ((TOKENS, width), bf16), ((TOKENS, width), f32), (packed.shape, bf16),
            ((layer_count, 8 + hidden // width + 4, width), f32),
            ((layer_count, head_count * SLOT, SLOT), f32),
        ],
        [
            ((layer_count + 1, TOKENS, width), f32), ((TOKENS, width), f32),
            kept(width, bf16), kept(3 * width, bf16), kept(width, bf16), kept(width, f32),
            kept(width, bf16), kept(hidden, f32), kept(hidden, bf16),
            ((TOKENS, width), bf16), ((TOKENS, 3 * width), bf16),
        ],
        [to_slots(images), to_slots(cotangent), packed, vec, fb, score_bias, region_mask, perm],
        flops,
        "both_blocks",
    )
    vec_part = small[:, :8].reshape(layer_count, 8, shard_count, rows).transpose(2, 0, 1, 3)
    vec_part = vec_part.reshape(shard_count, layer_count, 8 * rows)
    fb_part = small[:, 8 : 8 + hidden // width].reshape(layer_count, shard_count, hidden_own)
    small = jnp.concatenate([vec_part, jnp.swapaxes(fb_part, 0, 1)], axis=2)
    entries = rel_table.shape[1]
    entries_own = -(-entries // shard_count)
    table_terms = tables.reshape(layer_count, head_count, SLOT * SLOT)
    table_grad = lax.dot_general(
        onehot.astype(f32), table_terms, (((0,), (2,)), ((), ())), precision=highest
    )
    table_grad = jnp.pad(table_grad, ((0, entries_own * shard_count - entries), (0, 0), (0, 0)))
    table_grad = table_grad.reshape(shard_count, entries_own, layer_count, head_count)
    table_grad = jnp.swapaxes(table_grad, 1, 2).reshape(shard_count, layer_count, -1)

    def widen(part):
        return jnp.pad(low(part), ((0, 0), (0, 0), (0, width - part.shape[2])))

    tail = jnp.concatenate([widen(small), widen(table_grad)], axis=1)
    tail = jnp.pad(tail, ((0, 0), (0, PAD_ROWS - tail.shape[1]), (0, 0)))
    weight_grads = lax.dynamic_update_slice(
        weight_grads, tail, (0, packed.shape[1] - PAD_ROWS, 0)
    )
    share = lax.psum_scatter(weight_grads, "shard", scatter_dimension=0, tiled=False)
    total = rep_sum(share, rep_count)
    first = total.shape[0] - PAD_ROWS + layer_count
    table_own = total[first : first + layer_count, : entries_own * head_count]
    table_all = lax.all_gather(table_own, "shard", axis=0, tiled=False)
    table_all = table_all.reshape(shard_count, layer_count, entries_own, head_count)
    table_total = jnp.swapaxes(table_all, 0, 1).reshape(layer_count, -1, head_count)
    return (
        from_slots(out),
        from_slots(upstream),
        *unpack_shares(total, w_qkv, w_fc2, fc1_bias),
        table_total[:, :entries],
    )


def solution(mesh):
    return jax.shard_map(
        functools.partial(
            body, rep_count=mesh.shape["rep"], shard_count=mesh.shape["shard"]
        ),
        mesh=mesh,
        in_specs=(
            P(("rep", "shard"), None, None, None),
            P(("rep", "shard"), None, None, None),
            P(("rep", "shard"), None, None),
            P(None, "shard", None),
            P(None, "shard", None),
            P(None, "shard", None),
            P(None, "shard", None),
            P(None, None, "shard"),
            P(None, None, "shard"),
            P(None, None, "shard"),
            P(None, "shard"),
            P(),
        ),
        out_specs=(
            P(("rep", "shard"), None, None, None),
            P(("rep", "shard"), None, None, None),
            P(None, "shard", None),
            P(None, "shard", None),
            P(None, "shard", None),
            P(None, "shard", None),
            P(None, None, "shard"),
            P(None, None, "shard"),
            P(None, None, "shard"),
            P(None, "shard"),
            P(),
        ),
        check_vma=False,
    )
```
